32 devices in a mesh: groups: 2 (over y), expert: 4 (over x, core), replica: 4 (over z).
Axes of the slice: x: 2, y: 2, z: 4, core: 2. Of those that a mesh axis runs over, the one named last changes fastest.
Arguments:
- tokens: bfloat16 [8192, 2048], P(('groups', 'expert', 'replica')), parts along dimension 0, may hold values from -6 to 6
- norm_gain: float32 [2048], replicated, may hold values from 0.1 to 1.9
- router: bfloat16 [2048, 16], replicated, may hold values from -0.125 to 0.125
- down_proj: bfloat16 [2048, 512], P(('expert', 'replica')), may hold values from -0.125 to 0.125
- up_proj: bfloat16 [2048, 512], P(('expert', 'replica')), may hold values from -0.25 to 0.25
- expert_gate: bfloat16 [16, 512, 768], P('expert'), may hold values from -0.25 to 0.25
- expert_up: bfloat16 [16, 512, 768], P('expert'), may hold values from -0.25 to 0.25
- expert_down: bfloat16 [16, 768, 512], P('expert'), may hold values from -0.21875 to 0.21875
- expert_ids: int32 [8192, 8], P(('groups', 'expert', 'replica')), parts along dimension 0, may hold values from 0 to 15, as said below
- slot_pos: int32 [8192, 8], P(('groups', 'expert', 'replica')), parts along dimension 0, may hold values from -1 to 127, as said below
- overflow_list: int32 [32, 4, 4, 4], P(('groups', 'expert', 'replica')), parts along dimension 0, may hold values from -1 to 2047, as said below
Outputs:
- mixed: bfloat16 [8192, 2048], P(('groups', 'expert', 'replica')), parts along dimension 0
The draws below stay inside these ranges and needn't reach their ends.
There are 2 independent parts, one for each index of `groups`. The reference program is written for one: setup_inputs(seed, part) draws one part's arguments, and reference() takes and returns one part's arrays. A program takes and returns all parts, laid end to end along the dimension named above; an argument that names none is the same for every part. Nothing has to cross between parts.
Inputs may be any that keep to these rules, and one draw needn't show every extreme that they name: `expert_ids`: the 8 ids of a token are distinct. `slot_pos`: within the 256 rows of one device, the choices of one expert that have a slot hold distinct slots 0, 1, 2, ... in row order, so at most 128 from one device to one expert; in every draw some expert gets all 128 slots from every device. `overflow_list`: an entry is a choice index t' * 8 + k of the source device's own rows whose expert is (destination index of the expert axis) * 4 + (local expert) and whose slot_pos is -1; each choice is listed at most once. In every draw some expert is listed at every copy by every source device.
All inputs are finite; a program needn't handle non-finite values.
Results may differ from the reference program's by a relative error of at most 0.0088.
Values may be sent and summed in bfloat16 or wider, within the bound.
A program may use at most 128 MiB of HBM per device.

```python
import jax
import jax.numpy as jnp
from jax import lax

D = 2048
LATENT = 512
EXPERT_FF = 768
TOPK = 8
EXP_DEV = 4
TOK_DEV = 256
EXPERT_SHARDS = 4
COPIES = 4
SOURCES = 16
SPECIALIST_COUNT = 16
CAP = 128
TOKENS = 4096


def place_entries(table, cells, entries):
    return table.at[cells].set(entries, mode='drop')


def routing_tables(key):
    base = jax.random.fold_in(key, 11)
    k_hot, k_pop, k_noise, k_shift = jax.random.split(base, 4)
    busiest_specialist = jax.random.randint(k_hot, (), 0, SPECIALIST_COUNT)
    favored_specialist = jax.random.randint(k_pop, (SPECIALIST_COUNT,), 0, 4 * SPECIALIST_COUNT)
    gating_jitter = jax.random.randint(k_noise, (SOURCES, TOK_DEV, SPECIALIST_COUNT), 0, 8 * SPECIALIST_COUNT)
    shifts = jax.random.randint(k_shift, (SOURCES, 1), 0, TOK_DEV)
    places = jnp.arange(TOK_DEV, dtype=jnp.int32)[None, :]
    imposed_selection = (places + shifts) % TOK_DEV < CAP + COPIES
    feature_band = jnp.arange(SPECIALIST_COUNT, dtype=jnp.int32)
    extra_preference = jnp.where(imposed_selection[:, :, None] & (feature_band == busiest_specialist)[None, None, :], 16 * SPECIALIST_COUNT, 0)
    gating_affinity = (favored_specialist[None, None, :] + gating_jitter + extra_preference) * SPECIALIST_COUNT + feature_band
    _, chosen = lax.top_k(gating_affinity, TOPK)
    chosen = chosen.astype(jnp.int32)
    flat = chosen.reshape(SOURCES, TOK_DEV * TOPK)
    onehot = (flat[:, :, None] == feature_band[None, None, :]).astype(jnp.int32)
    before = jnp.cumsum(onehot, axis=1) - onehot
    rank = jnp.sum(before * onehot, axis=2)
    slots = jnp.where(rank < CAP, rank, -1).astype(jnp.int32)
    spill = rank - CAP
    owner = (jnp.arange(SOURCES, dtype=jnp.int32) % COPIES)[:, None]
    target = (owner + 1 + spill) % COPIES
    valid = (spill >= 0) & (spill < COPIES)
    cells = jnp.where(valid, flat * COPIES + target, SPECIALIST_COUNT * COPIES).astype(jnp.int32)
    entries = jnp.broadcast_to(jnp.arange(TOK_DEV * TOPK, dtype=jnp.int32)[None, :], flat.shape)
    table = jnp.full((SOURCES, SPECIALIST_COUNT * COPIES), -1, jnp.int32)
    table = jax.vmap(place_entries)(table, cells, entries)
    table = table.reshape(SOURCES, EXPERT_SHARDS, EXP_DEV, COPIES).transpose(0, 1, 3, 2)
    return (chosen.reshape(TOKENS, TOPK), slots.reshape(TOKENS, TOPK), table)


def draw_expert_ids(key, part):
    return routing_tables(key)[0]


def draw_slot_pos(key, part):
    return routing_tables(key)[1]


def draw_overflow_list(key, part):
    return routing_tables(key)[2]


def shard_levels(own_key, extent, shards, smallest, largest):
    def one(axis_at, blocks):
        draws = jax.random.uniform(jax.random.fold_in(jax.random.fold_in(own_key, 6), axis_at), (blocks,), jnp.float32, smallest / len(shards), largest / len(shards))
        return jnp.repeat(jnp.exp(draws), extent[axis_at] // blocks).reshape((-1,) + (1,) * (len(extent) - axis_at - 1))

    gain = one(*shards[0])
    for cut in shards[1:]:
        gain = gain * one(*cut)
    return gain


def normal_values(rng, extent, width, limit, pieces=(), kind=jnp.bfloat16):
    values = width * jax.random.normal(rng, extent, jnp.float32)
    if pieces:
        values = values * shard_levels(rng, extent, pieces, -0.22, 0.18)
    return jnp.clip(values, -limit, limit).astype(kind)


def setup_inputs(seed: int = 0, part: int = 0) -> dict:
    key_of = jax.random.split(jax.random.key(seed), 12)
    own_keys = jax.random.split(jax.random.fold_in(key_of[11], part), 12)
    tokens = normal_values(own_keys[0], (TOKENS, D), 1.0, 6.0, ((0, 16),))
    norm_gain = jnp.clip(1.0 + 0.18 * jax.random.normal(key_of[1], (D,), jnp.float32), 0.1, 1.9)
    router = normal_values(key_of[2], (D, SPECIALIST_COUNT), D ** -0.5, 0.125)
    down_proj = normal_values(key_of[3], (D, LATENT), D ** -0.5, 0.125, ((0, 16),))
    up_proj = normal_values(key_of[4], (D, LATENT), LATENT ** -0.5, 0.25, ((0, 16),))
    expert_gate = normal_values(key_of[5], (SPECIALIST_COUNT, LATENT, EXPERT_FF), LATENT ** -0.5, 0.25, ((0, 4),))
    expert_up = normal_values(key_of[6], (SPECIALIST_COUNT, LATENT, EXPERT_FF), LATENT ** -0.5, 0.25, ((0, 4),))
    expert_down = normal_values(key_of[7], (SPECIALIST_COUNT, EXPERT_FF, LATENT), EXPERT_FF ** -0.5, 0.21875, ((0, 4),))
    expert_ids = draw_expert_ids(jax.random.fold_in(jax.random.fold_in(key_of[11], part), 71), part)
    slot_pos = draw_slot_pos(jax.random.fold_in(jax.random.fold_in(key_of[11], part), 71), part)
    overflow_list = draw_overflow_list(jax.random.fold_in(jax.random.fold_in(key_of[11], part), 71), part)
    return dict(tokens=tokens, norm_gain=norm_gain, router=router, down_proj=down_proj, up_proj=up_proj, expert_gate=expert_gate, expert_up=expert_up, expert_down=expert_down, expert_ids=expert_ids, slot_pos=slot_pos, overflow_list=overflow_list)


epsilon = 1e-06

def reference(tokens, norm_gain, router, down_proj, up_proj, expert_gate, expert_up, expert_down, expert_ids, slot_pos, overflow_list):
    values = tokens.astype(jnp.float32)
    scaled = values * lax.rsqrt(lax.optimization_barrier(jnp.mean(values * values, axis=-1, keepdims=True)) + epsilon)
    normed = (scaled * norm_gain).astype(jnp.bfloat16)
    latent = jnp.dot(normed, down_proj, preferred_element_type=jnp.float32).astype(jnp.bfloat16)
    logits = jnp.dot(normed, router, preferred_element_type=jnp.float32)
    chosen = jnp.take_along_axis(logits, expert_ids, axis=1)
    sigmas = jax.nn.sigmoid(chosen)
    gates = (sigmas / lax.optimization_barrier(jnp.sum(sigmas, axis=1, keepdims=True))).reshape(-1)
    per_source = TOK_DEV * TOPK
    assign = jnp.arange(TOKENS * TOPK, dtype=jnp.int32)
    source = assign // per_source
    flat_ids = expert_ids.reshape(-1).astype(jnp.int32)
    flat_pos = slot_pos.reshape(-1).astype(jnp.int32)
    slot_index = jnp.where(flat_pos >= 0, (source * SPECIALIST_COUNT + flat_ids) * CAP + flat_pos, SOURCES * SPECIALIST_COUNT * CAP)
    first_list = jnp.full((SOURCES * SPECIALIST_COUNT * CAP,), -1, jnp.int32).at[slot_index].set(assign, mode='drop')
    first_list = first_list.reshape(SOURCES, SPECIALIST_COUNT, CAP).transpose(1, 0, 2).reshape(SPECIALIST_COUNT, SOURCES * CAP)
    offsets = (jnp.arange(SOURCES, dtype=jnp.int32) * per_source)[:, None, None, None]
    spare_list = jnp.where(overflow_list >= 0, overflow_list + offsets, -1).astype(jnp.int32)
    spare_list = spare_list.transpose(1, 3, 0, 2).reshape(SPECIALIST_COUNT, SOURCES * COPIES)
    row_lists = jnp.concatenate([first_list, spare_list], axis=1)

    def expert_step(combined, inputs):
        entries, w_gate, w_up, w_down = inputs
        valid = entries >= 0
        safe = jnp.maximum(entries, 0)
        rows = latent[safe // TOPK]
        gate = jnp.dot(rows, w_gate, preferred_element_type=jnp.float32)
        upper = jnp.dot(rows, w_up, preferred_element_type=jnp.float32)
        hidden = (jax.nn.silu(gate) * upper).astype(jnp.bfloat16)
        result = jnp.dot(hidden, w_down, preferred_element_type=jnp.float32).astype(jnp.bfloat16)
        weight = jnp.where(valid, gates[safe], jnp.zeros((), jnp.float32))
        combined = combined.at[safe // TOPK].add(result.astype(jnp.float32) * weight[:, None])
        return (combined, None)
    start = jnp.zeros((TOKENS, LATENT), jnp.float32)
    combined, _ = lax.scan(expert_step, start, (row_lists, expert_gate, expert_up, expert_down))
    merged = combined.astype(jnp.bfloat16)
    output = lax.dot_general(merged, up_proj, (((1,), (1,)), ((), ())), preferred_element_type=jnp.float32)
    return output.astype(jnp.bfloat16)
```

```python
import functools

import jax
import jax.numpy as jnp
from jax import lax
from jax.experimental import pallas as pl
from jax.experimental.pallas import tpu as pltpu
from jax.sharding import PartitionSpec as P

epsilon = 1e-06
CORES = 2
MESH = pl.DeviceIdType.MESH


def remote(src, dst, send, recv, where):
    return pltpu.make_async_remote_copy(
        src_ref=src, dst_ref=dst, send_sem=send, recv_sem=recv, device_id=where, device_id_type=MESH
    )


def layer(
    shards, copies, tok, gain, router, down, up, wg, wu, wd, ids, slot, ov, out,
    tokv, normed, dfull, ufull, gv, uv, dv, lat, wts, hid, acc, own, pbuf, rbuf,
    loc, dzs, dzr, dxs, dxr, dcs, dcr, uzs, uzr, uxs, uxr, ucs, ucr,
    lps, lpr, lxs, lxr, lfs, lfr, wps, wpr, wxs, wxr, wfs, wfr, rs, rr,
):
    columns = shards // CORES
    e, r = lax.axis_index("expert"), lax.axis_index("replica")
    x, c = e // CORES, e % CORES
    part = rows = down.shape[0]
    local = wg.shape[0]
    tokens = tok.shape[0]
    top = ids.shape[1]
    experts = router.shape[1]

    def ex(xx, cc):
        return xx * CORES + cc

    def back(d):
        return lax.rem(x - d + columns, columns)

    def fore(d):
        return lax.rem(x + d, columns)

    def zback(d):
        return lax.rem(r - d + copies, copies)

    def zdev(d):
        return {"replica": lax.rem(r + d, copies)}

    def xdev(d):
        return {"expert": ex(fore(d), c)}

    pdev = {"expert": ex(x, 1 - c)}

    def at(ref, index, n=1):
        return ref.at[pl.ds(pl.multiple_of(index * part, part), part * n), :]

    barrier = pltpu.get_barrier_semaphore()
    count = 1
    pl.semaphore_signal(barrier, inc=1, device_id=pdev, device_id_type=MESH)
    for d in range(1, copies):
        pl.semaphore_signal(barrier, inc=1, device_id=zdev(d), device_id_type=MESH)
        count += 1
    for d in range(1, columns):
        for cc in (c, 1 - c):
            pl.semaphore_signal(
                barrier, inc=1, device_id={"expert": ex(fore(d), cc)}, device_id_type=MESH
            )
            count += 1
    tcopy = pltpu.make_async_copy(tok, tokv, loc.at[0])
    mine = e * copies + r
    dcopy = pltpu.make_async_copy(down, at(dfull, mine), loc.at[1])
    ucopy = pltpu.make_async_copy(up, at(ufull, mine), loc.at[2])
    wcopies = [
        pltpu.make_async_copy(wg, gv, loc.at[3]),
        pltpu.make_async_copy(wu, uv, loc.at[4]),
        pltpu.make_async_copy(wd, dv, loc.at[5]),
    ]
    tcopy.start()
    dcopy.start()
    pl.semaphore_wait(barrier, count)

    sends = []

    def go(copy):
        copy.start()
        sends.append(copy)

    for d in range(1, columns):
        go(remote(down, at(dfull, mine), dxs.at[d - 1, 0], dxr.at[d - 1, 0], xdev(d)))
    for d in range(1, copies):
        go(remote(down, at(dfull, mine), dzs.at[d - 1], dzr.at[d - 1], zdev(d)))
    ucopy.start()
    for w in wcopies:
        w.start()

    tcopy.wait()
    step = 32

    @pl.loop(0, tokens // step)
    def _(i):
        at_rows = pl.ds(pl.multiple_of(i * step, step), step)
        v = tokv[at_rows, :].astype(jnp.float32)
        scaled = v * lax.rsqrt(jnp.mean(v * v, axis=-1, keepdims=True) + epsilon)
        normed[at_rows, :] = (scaled * gain[...]).astype(jnp.bfloat16)

    logits = jnp.dot(normed[...], router[...], preferred_element_type=jnp.float32)
    sig = 1.0 / (1.0 + jnp.exp(-logits))
    lane = lax.broadcasted_iota(jnp.int32, (tokens, experts), 1)
    row = lax.broadcasted_iota(jnp.int32, (tokens, experts), 0)
    chosen = jnp.zeros((tokens, experts), jnp.float32)
    served = jnp.zeros((tokens, experts), jnp.float32)
    for k in range(top):
        hit = lane == ids[:, k : k + 1]
        chosen = jnp.where(hit, 1.0, chosen)
        served = jnp.where(hit & (slot[:, k : k + 1] >= 0), 1.0, served)
    listed = jnp.concatenate([ov[0, d] for d in range(shards)], axis=1)
    for k in range(copies):
        entry = listed[k : k + 1, :]
        first = row * top
        served = jnp.where((entry >= first) & (entry < first + top), 1.0, served)
    weight = served * (sig / jnp.sum(chosen * sig, axis=1, keepdims=True))
    flipped = weight.T
    wts[e] = jnp.zeros(wts.shape[1:], jnp.float32)
    for d in range(shards):
        wts[e, d, 0:local, :] = flipped[d * local : (d + 1) * local, :]

    for j in range(1, copies):
        s = e * copies + zback(j)
        remote(down, at(dfull, s), dzs.at[j - 1], dzr.at[j - 1], zdev(j)).wait_recv()
        for d in range(1, columns):
            go(remote(at(dfull, s), at(dfull, s), dxs.at[d - 1, j], dxr.at[d - 1, j], xdev(d)))
    dcopy.wait()
    s = e * copies
    go(remote(at(dfull, s, copies), at(dfull, s, copies), dcs.at[0], dcr.at[0], pdev))
    for d in range(1, columns):
        go(remote(up, at(ufull, mine), uxs.at[d - 1], uxr.at[d - 1], xdev(d)))
    ucopy.wait()
    for z in range(1, copies):
        go(remote(at(ufull, mine), at(ufull, mine), uzs.at[z - 1, 0], uzr.at[z - 1, 0], zdev(z)))
    for d in range(1, columns):
        base = ex(back(d), c) * copies
        for j in range(copies):
            s = base + zback(j)
            remote(at(dfull, s), at(dfull, s), dxs.at[d - 1, j], dxr.at[d - 1, j], xdev(d)).wait_recv()
        go(remote(at(dfull, base, copies), at(dfull, base, copies), dcs.at[d], dcr.at[d], pdev))
    for d in range(columns):
        s = ex(back(d), 1 - c) * copies
        remote(at(dfull, s, copies), at(dfull, s, copies), dcs.at[d], dcr.at[d], pdev).wait_recv()

    lat[e] = jnp.dot(normed[...], dfull[...], preferred_element_type=jnp.float32).astype(jnp.bfloat16)
    for d in range(1, columns):
        go(remote(lat.at[e], lat.at[e], lxs.at[d - 1], lxr.at[d - 1], xdev(d)))
        go(remote(wts.at[e], wts.at[e], wxs.at[d - 1], wxr.at[d - 1], xdev(d)))
    go(remote(lat.at[e], lat.at[e], lps, lpr, pdev))
    go(remote(wts.at[e], wts.at[e], wps, wpr, pdev))

    width = wg.shape[2]
    piece = 256

    def experts_on(which):
        scale = wts[which, e].T
        spot = lax.broadcasted_iota(jnp.int32, scale.shape, 1)
        acc[...] = jnp.zeros_like(acc)

        @pl.loop(0, local)
        def _(n):
            block = lat[which]
            weights = jnp.sum(jnp.where(spot == n, scale, 0.0), axis=1, keepdims=True)
            for f in range(0, width, piece):
                a = jnp.dot(block, gv[n, :, f : f + piece], preferred_element_type=jnp.float32)
                b = jnp.dot(block, uv[n, :, f : f + piece], preferred_element_type=jnp.float32)
                h = a / (1.0 + jnp.exp(-a)) * b * weights
                hid[:, f : f + piece] = h.astype(jnp.bfloat16)
            acc[...] += jnp.dot(hid[...], dv[n], preferred_element_type=jnp.float32)

    for w in wcopies:
        w.wait()
    experts_on(e)
    own[...] = acc[...]
    for d in range(1, columns):
        s = ex(back(d), c) * copies + r
        remote(up, at(ufull, s), uxs.at[d - 1], uxr.at[d - 1], xdev(d)).wait_recv()
        for z in range(1, copies):
            go(remote(at(ufull, s), at(ufull, s), uzs.at[z - 1, d], uzr.at[z - 1, d], zdev(z)))
    p = ex(x, 1 - c)
    remote(lat.at[p], lat.at[p], lps, lpr, pdev).wait_recv()
    remote(wts.at[p], wts.at[p], wps, wpr, pdev).wait_recv()
    experts_on(p)
    pbuf[p] = acc[...].astype(jnp.bfloat16)
    go(remote(pbuf.at[p], rbuf.at[0], rs.at[0], rr.at[0], pdev))
    for d in range(1, columns):
        q = ex(back(d), c)
        remote(lat.at[q], lat.at[q], lxs.at[d - 1], lxr.at[d - 1], xdev(d)).wait_recv()
        remote(wts.at[q], wts.at[q], wxs.at[d - 1], wxr.at[d - 1], xdev(d)).wait_recv()
        go(remote(lat.at[q], lat.at[q], lfs.at[d - 1], lfr.at[d - 1], pdev))
        go(remote(wts.at[q], wts.at[q], wfs.at[d - 1], wfr.at[d - 1], pdev))
        experts_on(q)
        pbuf[q] = acc[...].astype(jnp.bfloat16)
        k = 2 * d - 1
        go(remote(pbuf.at[q], rbuf.at[k], rs.at[k], rr.at[k], {"expert": q}))
        q = ex(back(d), 1 - c)
        remote(lat.at[q], lat.at[q], lfs.at[d - 1], lfr.at[d - 1], pdev).wait_recv()
        remote(wts.at[q], wts.at[q], wfs.at[d - 1], wfr.at[d - 1], pdev).wait_recv()
        experts_on(q)
        pbuf[q] = acc[...].astype(jnp.bfloat16)
        k = 2 * d
        go(remote(pbuf.at[q], rbuf.at[k], rs.at[k], rr.at[k], {"expert": q}))

    for d in range(columns):
        base = ex(back(d), c) * copies
        for z in range(1, copies):
            s = base + zback(z)
            remote(at(ufull, s), at(ufull, s), uzs.at[z - 1, d], uzr.at[z - 1, d], zdev(z)).wait_recv()
        go(remote(at(ufull, base, copies), at(ufull, base, copies), ucs.at[d], ucr.at[d], pdev))
    for d in range(columns):
        s = ex(back(d), 1 - c) * copies
        remote(at(ufull, s, copies), at(ufull, s, copies), ucs.at[d], ucr.at[d], pdev).wait_recv()
    for k in range(shards - 1):
        remote(rbuf.at[k], rbuf.at[k], rs.at[k], rr.at[k], pdev).wait_recv()
        own[...] += rbuf[k].astype(jnp.float32)
    out[...] = lax.dot_general(
        own[...].astype(jnp.bfloat16), ufull[...], (((1,), (1,)), ((), ())),
        preferred_element_type=jnp.float32,
    ).astype(jnp.bfloat16)
    for copy in sends:
        copy.wait_send()


def on_device(
    tokens, norm_gain, router, down_proj, up_proj, expert_gate, expert_up, expert_down,
    expert_ids, slot_pos, overflow_list,
):
    shards, copies = lax.axis_size("expert"), lax.axis_size("replica")
    columns = shards // CORES
    rows, width = tokens.shape
    latent = down_proj.shape[1]
    bf, f32 = jnp.bfloat16, jnp.float32
    dma = pltpu.SemaphoreType.DMA
    more = max(columns - 1, 1)
    extra = max(copies - 1, 1)
    anywhere, vmem = pl.BlockSpec(memory_space=pl.ANY), pl.BlockSpec(memory_space=pltpu.VMEM)
    return pl.pallas_call(
        functools.partial(layer, shards, copies),
        out_shape=jax.ShapeDtypeStruct((rows, width), bf),
        in_specs=[anywhere, vmem, vmem] + [anywhere] * 5 + [vmem] * 3,
        out_specs=vmem,
        scratch_shapes=[
            pltpu.VMEM((rows, width), bf),
            pltpu.VMEM((rows, width), bf),
            pltpu.VMEM((width, latent), bf),
            pltpu.VMEM((width, latent), bf),
            pltpu.VMEM(expert_gate.shape, bf),
            pltpu.VMEM(expert_up.shape, bf),
            pltpu.VMEM(expert_down.shape, bf),
            pltpu.VMEM((shards, rows, latent), bf),
            pltpu.VMEM((shards, shards, pl.cdiv(expert_gate.shape[0], 8) * 8, rows), f32),
            pltpu.VMEM((rows, expert_gate.shape[2]), bf),
            pltpu.VMEM((rows, latent), f32),
            pltpu.VMEM((rows, latent), f32),
            pltpu.VMEM((shards, rows, latent), bf),
            pltpu.VMEM((shards - 1, rows, latent), bf),
            dma((6,)),
            dma((extra,)), dma((extra,)),
            dma((more, copies)), dma((more, copies)),
            dma((columns,)), dma((columns,)),
            dma((extra, columns)), dma((extra, columns)),
            dma((more,)), dma((more,)),
            dma((columns,)), dma((columns,)),
            dma, dma, dma((more,)), dma((more,)), dma((more,)), dma((more,)),
            dma, dma, dma((more,)), dma((more,)), dma((more,)), dma((more,)),
            dma((shards - 1,)), dma((shards - 1,)),
        ],
        compiler_params=pltpu.CompilerParams(collective_id=0, has_side_effects=True,
                                             vmem_limit_bytes=60 * 1024 * 1024),
    )(
        tokens, norm_gain.reshape(1, -1), router, down_proj, up_proj, expert_gate, expert_up,
        expert_down, expert_ids, slot_pos, overflow_list,
    )


def solution(mesh):
    placed = (
        P(("groups", "expert", "replica"), None),
        P(),
        P(),
        P(("expert", "replica"), None),
        P(("expert", "replica"), None),
        P("expert", None, None),
        P("expert", None, None),
        P("expert", None, None),
        P(("groups", "expert", "replica"), None),
        P(("groups", "expert", "replica"), None),
        P(("groups", "expert", "replica"), None, None, None),
    )
    return jax.shard_map(
        on_device,
        mesh=mesh,
        in_specs=placed,
        out_specs=P(("groups", "expert", "replica"), None),
        check_vma=False,
    )
```

```python
import functools

import jax
import jax.numpy as jnp
from jax import lax
from jax.experimental import pallas as pl
from jax.experimental.pallas import tpu as pltpu
from jax.sharding import PartitionSpec as P

epsilon = 1e-06
CORES = 2
MESH = pl.DeviceIdType.MESH


def remote(src, dst, send, recv, where):
    return pltpu.make_async_remote_copy(
        src_ref=src, dst_ref=dst, send_sem=send, recv_sem=recv, device_id=where, device_id_type=MESH
    )


def layer(
    teams, shards, copies, tok, gain, router, down, up, wg, wu, wd, ids, slot, ov, out,
    tokv, normed, dfull, ufull, gv, uv, dv, lat, wts, hid, acc, own, pbuf, rbuf,
    loc, dzs, dzr, dxs, dxr, dcs, dcr, uzs, uzr, uxs, uxr, ucs, ucr,
    uys, uyr, lps, lpr, lxs, lxr, lfs, lfr, wps, wpr, wxs, wxr, wfs, wfr, rs, rr,
):
    columns = shards // CORES
    g, e, r = lax.axis_index("groups"), lax.axis_index("expert"), lax.axis_index("replica")
    x, c = e // CORES, e % CORES
    part = rows = down.shape[0]
    local = wg.shape[0]
    tokens = tok.shape[0]
    top = ids.shape[0]
    experts = router.shape[0]

    def ex(xx, cc):
        return xx * CORES + cc

    def back(d):
        return lax.rem(x - d + columns, columns)

    def fore(d):
        return lax.rem(x + d, columns)

    def zback(d):
        return lax.rem(r - d + copies, copies)

    def zdev(d):
        return {"replica": lax.rem(r + d, copies)}

    def xdev(d):
        return {"expert": ex(fore(d), c)}

    pdev = {"expert": ex(x, 1 - c)}

    def at(ref, index, n=1):
        return ref.at[pl.ds(pl.multiple_of(index * part, part), part * n), :]

    def ydev(d):
        return {"groups": lax.rem(g + d, teams)}

    share = up.shape[1] // teams

    def slab(ref, index, team, n=1):
        return ref.at[
            pl.ds(pl.multiple_of(index * part, part), part * n),
            pl.ds(pl.multiple_of(team * share, share), share),
        ]

    barrier = pltpu.get_barrier_semaphore()
    count = 1
    pl.semaphore_signal(barrier, inc=1, device_id=pdev, device_id_type=MESH)
    for d in range(1, copies):
        pl.semaphore_signal(barrier, inc=1, device_id=zdev(d), device_id_type=MESH)
        count += 1
    for d in range(1, teams):
        pl.semaphore_signal(barrier, inc=1, device_id=ydev(d), device_id_type=MESH)
        count += 1
    for d in range(1, columns):
        for cc in (c, 1 - c):
            pl.semaphore_signal(
                barrier, inc=1, device_id={"expert": ex(fore(d), cc)}, device_id_type=MESH
            )
            count += 1
    tcopy = pltpu.make_async_copy(tok, tokv, loc.at[0])
    mine = e * copies + r
    dcopy = pltpu.make_async_copy(down, at(dfull, mine), loc.at[1])
    ucopy = pltpu.make_async_copy(slab(up, 0, g), slab(ufull, mine, g), loc.at[2])
    wcopies = [
        pltpu.make_async_copy(wg, gv, loc.at[3]),
        pltpu.make_async_copy(wu, uv, loc.at[4]),
        pltpu.make_async_copy(wd, dv, loc.at[5]),
    ]
    tcopy.start()
    dcopy.start()
    pl.semaphore_wait(barrier, count)

    sends = []

    def go(copy):
        copy.start()
        sends.append(copy)

    for d in range(1, columns):
        go(remote(down, at(dfull, mine), dxs.at[d - 1, 0], dxr.at[d - 1, 0], xdev(d)))
    for d in range(1, copies):
        go(remote(down, at(dfull, mine), dzs.at[d - 1], dzr.at[d - 1], zdev(d)))
    ucopy.start()
    for w in wcopies:
        w.start()

    tcopy.wait()
    step = 32

    @pl.loop(0, tokens // step)
    def _(i):
        at_rows = pl.ds(pl.multiple_of(i * step, step), step)
        v = tokv[at_rows, :].astype(jnp.float32)
        scaled = v * lax.rsqrt(jnp.mean(v * v, axis=-1, keepdims=True) + epsilon)
        normed[at_rows, :] = (scaled * gain[...]).astype(jnp.bfloat16)

    logits = lax.dot_general(
        router[...], normed[...], (((1,), (1,)), ((), ())), preferred_element_type=jnp.float32
    )
    sig = 1.0 / (1.0 + jnp.exp(-logits))
    expert = lax.broadcasted_iota(jnp.int32, (experts, tokens), 0)
    first = lax.broadcasted_iota(jnp.int32, (experts, tokens), 1) * top
    chosen = jnp.zeros((experts, tokens), jnp.float32)
    served = jnp.zeros((experts, tokens), jnp.float32)
    for k in range(top):
        hit = expert == ids[k : k + 1, :]
        chosen = jnp.where(hit, 1.0, chosen)
        served = jnp.where(hit & (slot[k : k + 1, :] >= 0), 1.0, served)
    listed = jnp.concatenate([ov[0, d] for d in range(shards)], axis=1).T
    for k in range(copies):
        entry = listed[:, k : k + 1]
        served = jnp.where((entry >= first) & (entry < first + top), 1.0, served)
    flipped = served * (sig / jnp.sum(chosen * sig, axis=0, keepdims=True))
    wts[e] = jnp.zeros(wts.shape[1:], jnp.float32)
    for d in range(shards):
        wts[e, d, 0:local, :] = flipped[d * local : (d + 1) * local, :]

    for j in range(1, copies):
        s = e * copies + zback(j)
        remote(down, at(dfull, s), dzs.at[j - 1], dzr.at[j - 1], zdev(j)).wait_recv()
        for d in range(1, columns):
            go(remote(at(dfull, s), at(dfull, s), dxs.at[d - 1, j], dxr.at[d - 1, j], xdev(d)))
    dcopy.wait()
    s = e * copies
    go(remote(at(dfull, s, copies), at(dfull, s, copies), dcs.at[0], dcr.at[0], pdev))
    for d in range(1, columns):
        go(remote(slab(up, 0, g), slab(ufull, mine, g), uxs.at[d - 1], uxr.at[d - 1], xdev(d)))
    ucopy.wait()
    for z in range(1, copies):
        here = slab(ufull, mine, g)
        go(remote(here, here, uzs.at[z - 1, 0], uzr.at[z - 1, 0], zdev(z)))
    for d in range(1, columns):
        base = ex(back(d), c) * copies
        for j in range(copies):
            s = base + zback(j)
            remote(at(dfull, s), at(dfull, s), dxs.at[d - 1, j], dxr.at[d - 1, j], xdev(d)).wait_recv()
        go(remote(at(dfull, base, copies), at(dfull, base, copies), dcs.at[d], dcr.at[d], pdev))
    for d in range(columns):
        s = ex(back(d), 1 - c) * copies
        remote(at(dfull, s, copies), at(dfull, s, copies), dcs.at[d], dcr.at[d], pdev).wait_recv()

    lat[e] = jnp.dot(normed[...], dfull[...], preferred_element_type=jnp.float32).astype(jnp.bfloat16)
    for d in range(1, columns):
        go(remote(lat.at[e], lat.at[e], lxs.at[d - 1], lxr.at[d - 1], xdev(d)))
        go(remote(wts.at[e], wts.at[e], wxs.at[d - 1], wxr.at[d - 1], xdev(d)))
    go(remote(lat.at[e], lat.at[e], lps, lpr, pdev))
    go(remote(wts.at[e], wts.at[e], wps, wpr, pdev))

    for d in range(1, columns):
        here = slab(ufull, ex(back(d), c) * copies + r, g)
        remote(here, here, uxs.at[d - 1], uxr.at[d - 1], xdev(d)).wait_recv()
        for z in range(1, copies):
            go(remote(here, here, uzs.at[z - 1, d], uzr.at[z - 1, d], zdev(z)))

    def up_across(d):
        base = ex(back(d), c) * copies
        for z in range(1, copies):
            here = slab(ufull, base + zback(z), g)
            remote(here, here, uzs.at[z - 1, d], uzr.at[z - 1, d], zdev(z)).wait_recv()
        here = slab(ufull, base, g, copies)
        for y in range(1, teams):
            go(remote(here, here, uys.at[y - 1, d], uyr.at[y - 1, d], ydev(y)))

    width = wg.shape[2]
    piece = 256

    def experts_on(which):
        scale = wts[which, e].T
        spot = lax.broadcasted_iota(jnp.int32, scale.shape, 1)
        acc[...] = jnp.zeros_like(acc)

        @pl.loop(0, local)
        def _(n):
            block = lat[which]
            weights = jnp.sum(jnp.where(spot == n, scale, 0.0), axis=1, keepdims=True)
            for f in range(0, width, piece):
                a = jnp.dot(block, gv[n, :, f : f + piece], preferred_element_type=jnp.float32)
                b = jnp.dot(block, uv[n, :, f : f + piece], preferred_element_type=jnp.float32)
                h = a / (1.0 + jnp.exp(-a)) * b * weights
                hid[:, f : f + piece] = h.astype(jnp.bfloat16)
            acc[...] += jnp.dot(hid[...], dv[n], preferred_element_type=jnp.float32)

    for w in wcopies:
        w.wait()
    experts_on(e)
    own[...] = acc[...]
    p = ex(x, 1 - c)
    remote(lat.at[p], lat.at[p], lps, lpr, pdev).wait_recv()
    remote(wts.at[p], wts.at[p], wps, wpr, pdev).wait_recv()
    experts_on(p)
    up_across(0)
    pbuf[p] = acc[...].astype(jnp.bfloat16)
    go(remote(pbuf.at[p], rbuf.at[0], rs.at[0], rr.at[0], pdev))
    for d in range(1, columns):
        q = ex(back(d), c)
        remote(lat.at[q], lat.at[q], lxs.at[d - 1], lxr.at[d - 1], xdev(d)).wait_recv()
        remote(wts.at[q], wts.at[q], wxs.at[d - 1], wxr.at[d - 1], xdev(d)).wait_recv()
        go(remote(lat.at[q], lat.at[q], lfs.at[d - 1], lfr.at[d - 1], pdev))
        go(remote(wts.at[q], wts.at[q], wfs.at[d - 1], wfr.at[d - 1], pdev))
        experts_on(q)
        pbuf[q] = acc[...].astype(jnp.bfloat16)
        k = 2 * d - 1
        go(remote(pbuf.at[q], rbuf.at[k], rs.at[k], rr.at[k], {"expert": q}))
        q = ex(back(d), 1 - c)
        remote(lat.at[q], lat.at[q], lfs.at[d - 1], lfr.at[d - 1], pdev).wait_recv()
        remote(wts.at[q], wts.at[q], wfs.at[d - 1], wfr.at[d - 1], pdev).wait_recv()
        experts_on(q)
        pbuf[q] = acc[...].astype(jnp.bfloat16)
        up_across(d)
        k = 2 * d
        go(remote(pbuf.at[q], rbuf.at[k], rs.at[k], rr.at[k], {"expert": q}))

    for d in range(columns):
        base = ex(back(d), c) * copies
        for y in range(1, teams):
            here = slab(ufull, base, lax.rem(g - y + teams, teams), copies)
            remote(here, here, uys.at[y - 1, d], uyr.at[y - 1, d], ydev(y)).wait_recv()
        go(remote(at(ufull, base, copies), at(ufull, base, copies), ucs.at[d], ucr.at[d], pdev))
    for d in range(columns):
        s = ex(back(d), 1 - c) * copies
        remote(at(ufull, s, copies), at(ufull, s, copies), ucs.at[d], ucr.at[d], pdev).wait_recv()
    for k in range(shards - 1):
        remote(rbuf.at[k], rbuf.at[k], rs.at[k], rr.at[k], pdev).wait_recv()
        own[...] += rbuf[k].astype(jnp.float32)
    out[...] = lax.dot_general(
        own[...].astype(jnp.bfloat16), ufull[...], (((1,), (1,)), ((), ())),
        preferred_element_type=jnp.float32,
    ).astype(jnp.bfloat16)
    for copy in sends:
        copy.wait_send()


def on_device(
    tokens, norm_gain, router, down_proj, up_proj, expert_gate, expert_up, expert_down,
    expert_ids, slot_pos, overflow_list,
):
    shards, copies = lax.axis_size("expert"), lax.axis_size("replica")
    teams = lax.axis_size("groups")
    columns = shards // CORES
    rows, width = tokens.shape
    latent = down_proj.shape[1]
    bf, f32 = jnp.bfloat16, jnp.float32
    dma = pltpu.SemaphoreType.DMA
    more = max(columns - 1, 1)
    extra = max(copies - 1, 1)
    anywhere, vmem = pl.BlockSpec(memory_space=pl.ANY), pl.BlockSpec(memory_space=pltpu.VMEM)
    return pl.pallas_call(
        functools.partial(layer, teams, shards, copies),
        out_shape=jax.ShapeDtypeStruct((rows, width), bf),
        in_specs=[anywhere, vmem, vmem] + [anywhere] * 5 + [vmem] * 3,
        out_specs=vmem,
        scratch_shapes=[
            pltpu.VMEM((rows, width), bf),
            pltpu.VMEM((rows, width), bf),
            pltpu.VMEM((width, latent), bf),
            pltpu.VMEM((width, latent), bf),
            pltpu.VMEM(expert_gate.shape, bf),
            pltpu.VMEM(expert_up.shape, bf),
            pltpu.VMEM(expert_down.shape, bf),
            pltpu.VMEM((shards, rows, latent), bf),
            pltpu.VMEM((shards, shards, pl.cdiv(expert_gate.shape[0], 8) * 8, rows), f32),
            pltpu.VMEM((rows, expert_gate.shape[2]), bf),
            pltpu.VMEM((rows, latent), f32),
            pltpu.VMEM((rows, latent), f32),
            pltpu.VMEM((shards, rows, latent), bf),
            pltpu.VMEM((shards - 1, rows, latent), bf),
            dma((6,)),
            dma((extra,)), dma((extra,)),
            dma((more, copies)), dma((more, copies)),
            dma((columns,)), dma((columns,)),
            dma((extra, columns)), dma((extra, columns)),
            dma((more,)), dma((more,)),
            dma((columns,)), dma((columns,)),
            dma((max(teams - 1, 1), columns)), dma((max(teams - 1, 1), columns)),
            dma, dma, dma((more,)), dma((more,)), dma((more,)), dma((more,)),
            dma, dma, dma((more,)), dma((more,)), dma((more,)), dma((more,)),
            dma((shards - 1,)), dma((shards - 1,)),
        ],
        compiler_params=pltpu.CompilerParams(collective_id=0, has_side_effects=True,
                                             vmem_limit_bytes=60 * 1024 * 1024),
    )(
        tokens, norm_gain.reshape(1, -1), router.T, down_proj, up_proj, expert_gate, expert_up,
        expert_down, expert_ids.T, slot_pos.T, overflow_list,
    )


def solution(mesh):
    placed = (
        P(("groups", "expert", "replica"), None),
        P(),
        P(),
        P(("expert", "replica"), None),
        P(("expert", "replica"), None),
        P("expert", None, None),
        P("expert", None, None),
        P("expert", None, None),
        P(("groups", "expert", "replica"), None),
        P(("groups", "expert", "replica"), None),
        P(("groups", "expert", "replica"), None, None, None),
    )
    return jax.shard_map(
        on_device,
        mesh=mesh,
        in_specs=placed,
        out_specs=P(("groups", "expert", "replica"), None),
        check_vma=False,
    )
```

```python
import functools

import jax
import jax.numpy as jnp
from jax import lax
from jax.experimental import pallas as pl
from jax.experimental.pallas import tpu as pltpu
from jax.sharding import PartitionSpec as P

epsilon = 1e-06
CORES = 2
MESH = pl.DeviceIdType.MESH


def remote(src, dst, send, recv, where):
    return pltpu.make_async_remote_copy(
        src_ref=src, dst_ref=dst, send_sem=send, recv_sem=recv, device_id=where, device_id_type=MESH
    )


def layer(
    teams, shards, copies, tok, gain, router, down, up, wg, wu, wd, ids, slot, ov, out,
    tokv, normed, dfull, ufull, gv, uv, dv, lat, wts, hid, acc, own, pbuf, rbuf,
    rows_in, gate, far, stage,
    loc, dzs, dzr, dxs, dxr, dcs, dcr, dys, dyr, uzs, uzr, uxs, uxr, ucs, ucr, uys, uyr,
    lps, lpr, lxs, lxr, lfs, lfr, wps, wpr, wxs, wxr, wfs, wfr, rs, rr, sts, str_,
):
    columns = shards // CORES
    g, e, r = lax.axis_index("groups"), lax.axis_index("expert"), lax.axis_index("replica")
    x, c = e // CORES, e % CORES
    part = rows = down.shape[0]
    local = wg.shape[0]
    tokens = tok.shape[0]
    top = ids.shape[0]
    experts = router.shape[0]

    def ex(xx, cc):
        return xx * CORES + cc

    def back(d):
        return lax.rem(x - d + columns, columns)

    def fore(d):
        return lax.rem(x + d, columns)

    def zback(d):
        return lax.rem(r - d + copies, copies)

    def zdev(d):
        return {"replica": lax.rem(r + d, copies)}

    def xdev(d):
        return {"expert": ex(fore(d), c)}

    pdev = {"expert": ex(x, 1 - c)}

    def at(ref, index, n=1):
        return ref.at[pl.ds(pl.multiple_of(index * part, part), part * n), :]

    def ydev(d):
        return {"groups": lax.rem(g + d, teams)}

    share = up.shape[1] // teams

    lent = part * 3 // 8 // 16 * 16 if teams == 2 else 0
    kept = part - lent

    def fetched(ref, index):
        return ref.at[pl.ds(pl.multiple_of(index * part + g * lent, 16), kept), :]

    def swapped(index, team):
        return dfull.at[pl.ds(pl.multiple_of(index * part + team * kept, 16), lent), :]

    def slab(ref, index, team, n=1):
        return ref.at[
            pl.ds(pl.multiple_of(index * part, part), part * n),
            pl.ds(pl.multiple_of(team * share, share), share),
        ]

    barrier = pltpu.get_barrier_semaphore()
    count = 1
    pl.semaphore_signal(barrier, inc=1, device_id=pdev, device_id_type=MESH)
    for d in range(1, copies):
        pl.semaphore_signal(barrier, inc=1, device_id=zdev(d), device_id_type=MESH)
        count += 1
    for d in range(1, teams):
        pl.semaphore_signal(barrier, inc=1, device_id=ydev(d), device_id_type=MESH)
        count += 1
    for d in range(1, columns):
        for cc in (c, 1 - c):
            pl.semaphore_signal(
                barrier, inc=1, device_id={"expert": ex(fore(d), cc)}, device_id_type=MESH
            )
            count += 1
    tcopy = pltpu.make_async_copy(tok, tokv, loc.at[0])
    mine = e * copies + r
    dcopy = pltpu.make_async_copy(down, at(dfull, mine), loc.at[1])
    ucopy = pltpu.make_async_copy(slab(up, 0, g), slab(ufull, mine, g), loc.at[2])
    wcopies = [
        pltpu.make_async_copy(wg, gv, loc.at[3]),
        pltpu.make_async_copy(wu, uv, loc.at[4]),
        pltpu.make_async_copy(wd, dv, loc.at[5]),
    ]
    tcopy.start()
    dcopy.start()
    pl.semaphore_wait(barrier, count)

    sends = []

    def go(copy):
        copy.start()
        sends.append(copy)

    for d in range(1, columns):
        go(remote(fetched(down, 0), fetched(dfull, mine), dxs.at[d - 1, 0], dxr.at[d - 1, 0], xdev(d)))
    for d in range(1, copies):
        go(remote(fetched(down, 0), fetched(dfull, mine), dzs.at[d - 1], dzr.at[d - 1], zdev(d)))
    go(remote(down, at(dfull, mine), dcs.at[0, 0, 0], dcr.at[0, 0, 0], pdev))
    ucopy.start()
    for w in wcopies:
        w.start()

    tcopy.wait()
    step = 32

    @pl.loop(0, tokens // step)
    def _(i):
        at_rows = pl.ds(pl.multiple_of(i * step, step), step)
        v = tokv[at_rows, :].astype(jnp.float32)
        scaled = v * lax.rsqrt(jnp.mean(v * v, axis=-1, keepdims=True) + epsilon)
        normed[at_rows, :] = (scaled * gain[...]).astype(jnp.bfloat16)

    logits = lax.dot_general(
        router[...], normed[...], (((1,), (1,)), ((), ())), preferred_element_type=jnp.float32
    )
    sig = 1.0 / (1.0 + jnp.exp(-logits))
    expert = lax.broadcasted_iota(jnp.int32, (experts, tokens), 0)
    first = lax.broadcasted_iota(jnp.int32, (experts, tokens), 1) * top
    chosen = jnp.zeros((experts, tokens), jnp.float32)
    served = jnp.zeros((experts, tokens), jnp.float32)
    for k in range(top):
        hit = expert == ids[k : k + 1, :]
        chosen = jnp.where(hit, 1.0, chosen)
        served = jnp.where(hit & (slot[k : k + 1, :] >= 0), 1.0, served)
    listed = jnp.concatenate([ov[0, d] for d in range(shards)], axis=1).T
    for k in range(copies):
        entry = listed[:, k : k + 1]
        served = jnp.where((entry >= first) & (entry < first + top), 1.0, served)
    flipped = served * (sig / jnp.sum(chosen * sig, axis=0, keepdims=True))
    wts[e] = jnp.zeros(wts.shape[1:], jnp.float32)
    for d in range(shards):
        wts[e, d, 0:local, :] = flipped[d * local : (d + 1) * local, :]

    def down_on(d, j):
        s = ex(back(d), c) * copies + zback(j)
        here = fetched(dfull, s)
        go(remote(here, here, dcs.at[d, j, 0], dcr.at[d, j, 0], pdev))
        if lent:
            here = swapped(s, g)
            go(remote(here, here, dys.at[d, j], dyr.at[d, j], ydev(1)))

    def down_z(j):
        here = fetched(dfull, e * copies + zback(j))
        remote(here, here, dzs.at[j - 1], dzr.at[j - 1], zdev(j)).wait_recv()
        for d in range(1, columns):
            go(remote(here, here, dxs.at[d - 1, j], dxr.at[d - 1, j], xdev(d)))
        down_on(0, j)

    def down_x(j):
        for d in range(1, columns):
            here = fetched(dfull, ex(back(d), c) * copies + zback(j))
            remote(here, here, dxs.at[d - 1, j], dxr.at[d - 1, j], xdev(d)).wait_recv()
            down_on(d, j)

    for j in range(1, copies):
        down_z(j)
        down_x(j - 1)
    for d in range(1, columns):
        go(remote(slab(up, 0, g), slab(ufull, mine, g), uxs.at[d - 1], uxr.at[d - 1], xdev(d)))
    ucopy.wait()
    for z in range(1, copies):
        here = slab(ufull, mine, g)
        go(remote(here, here, uzs.at[z - 1, 0], uzr.at[z - 1, 0], zdev(z)))
    down_x(copies - 1)
    others = [(d, j) for d in range(columns) for j in range(copies) if d + j]
    if lent:
        for d, j in others:
            here = swapped(ex(back(d), c) * copies + zback(j), 1 - g)
            remote(here, here, dys.at[d, j], dyr.at[d, j], ydev(1)).wait_recv()
            go(remote(here, here, dcs.at[d, j, 1], dcr.at[d, j, 1], pdev))
    dcopy.wait()
    here = at(dfull, ex(x, 1 - c) * copies + r)
    remote(here, here, dcs.at[0, 0, 0], dcr.at[0, 0, 0], pdev).wait_recv()
    for d, j in others:
        s = ex(back(d), 1 - c) * copies + zback(j)
        here = fetched(dfull, s)
        remote(here, here, dcs.at[d, j, 0], dcr.at[d, j, 0], pdev).wait_recv()
        if lent:
            here = swapped(s, 1 - g)
            remote(here, here, dcs.at[d, j, 1], dcr.at[d, j, 1], pdev).wait_recv()

    lat[e] = jnp.dot(normed[...], dfull[...], preferred_element_type=jnp.float32).astype(jnp.bfloat16)
    half = tokens // 2

    def half_of(ref, index, h):
        return ref.at[index, pl.ds(h * half, half), :]

    for d in range(1, columns):
        go(remote(wts.at[e], wts.at[e], wxs.at[d - 1], wxr.at[d - 1], xdev(d)))
        here = half_of(lat, e, 0)
        go(remote(here, here, lxs.at[d - 1, 0], lxr.at[d - 1, 0], xdev(d)))
    go(remote(wts.at[e], wts.at[e], wps, wpr, pdev))
    go(remote(lat.at[e], lat.at[e], lps, lpr, pdev))
    for d in range(1, columns):
        here = half_of(lat, e, 1)
        go(remote(here, here, lxs.at[d - 1, 1], lxr.at[d - 1, 1], xdev(d)))

    for d in range(1, columns):
        here = slab(ufull, ex(back(d), c) * copies + r, g)
        remote(here, here, uxs.at[d - 1], uxr.at[d - 1], xdev(d)).wait_recv()
        for z in range(1, copies):
            go(remote(here, here, uzs.at[z - 1, d], uzr.at[z - 1, d], zdev(z)))

    def up_across(d):
        base = ex(back(d), c) * copies
        for z in range(1, copies):
            here = slab(ufull, base + zback(z), g)
            remote(here, here, uzs.at[z - 1, d], uzr.at[z - 1, d], zdev(z)).wait_recv()
        here = slab(ufull, base, g, copies)
        for y in range(1, teams):
            go(remote(here, here, uys.at[y - 1, d], uyr.at[y - 1, d], ydev(y)))

    width = wg.shape[2]
    piece = 256

    def experts_on(pieces, middle):
        block = [lat[which, lo : lo + n, :] for which, lo, n in pieces]
        rows_in[...] = block[0] if len(block) == 1 else jnp.concatenate(block, axis=0)
        scale = [wts[which, e].T[lo : lo + n] for which, lo, n in pieces]
        gate[...] = scale[0] if len(scale) == 1 else jnp.concatenate(scale, axis=0)
        acc[...] = jnp.zeros_like(acc)

        def one(n):
            inner = rows_in[...]
            spot = lax.broadcasted_iota(jnp.int32, gate.shape, 1)
            weights = jnp.sum(jnp.where(spot == n, gate[...], 0.0), axis=1, keepdims=True)
            for f in range(0, width, piece):
                a = jnp.dot(inner, gv[n, :, f : f + piece], preferred_element_type=jnp.float32)
                b = jnp.dot(inner, uv[n, :, f : f + piece], preferred_element_type=jnp.float32)
                h = a / (1.0 + jnp.exp(-a)) * b * weights
                hid[:, f : f + piece] = h.astype(jnp.bfloat16)
            acc[...] += jnp.dot(hid[...], dv[n], preferred_element_type=jnp.float32)

        pl.loop(0, local // 2)(one)
        middle()
        pl.loop(local // 2, local)(one)

    def pass_on(h):
        for d in range(1, columns):
            q = ex(back(d), c)
            if h == 0:
                remote(wts.at[q], wts.at[q], wxs.at[d - 1], wxr.at[d - 1], xdev(d)).wait_recv()
                go(remote(wts.at[q], wts.at[q], wfs.at[d - 1], wfr.at[d - 1], pdev))
            here = half_of(lat, q, h)
            remote(here, here, lxs.at[d - 1, h], lxr.at[d - 1, h], xdev(d)).wait_recv()
            go(remote(here, here, lfs.at[d - 1, h], lfr.at[d - 1, h], pdev))

    for w in wcopies:
        w.wait()
    experts_on([(e, 0, tokens)], lambda: None)
    own[...] = acc[...]
    p = ex(x, 1 - c)
    remote(wts.at[p], wts.at[p], wps, wpr, pdev).wait_recv()
    remote(lat.at[p], lat.at[p], lps, lpr, pdev).wait_recv()
    experts_on([(p, 0, tokens)], lambda: pass_on(0))
    pbuf[p] = acc[...].astype(jnp.bfloat16)
    go(remote(pbuf.at[p], rbuf.at[0], rs.at[0, 0], rr.at[0, 0], pdev))
    up_across(0)

    def settle(d, h):
        span = slice(h * half, (h + 1) * half)
        q = ex(back(d), c)
        here = half_of(stage, d - 1, h)
        remote(here, here, sts.at[d - 1, h], str_.at[d - 1, h], pdev).wait_recv()
        total = far[h] + stage[d - 1, span, :].astype(jnp.float32)
        pbuf[q, span, :] = total.astype(jnp.bfloat16)
        go(remote(half_of(pbuf, q, h), half_of(rbuf, d, h), rs.at[d, h], rr.at[d, h], {"expert": q}))

    for d in range(1, columns):
        q, t = ex(back(d), c), ex(back(d), 1 - c)
        for h in range(2):
            if h == 0:
                remote(wts.at[t], wts.at[t], wfs.at[d - 1], wfr.at[d - 1], pdev).wait_recv()
            here = half_of(lat, t, h)
            remote(here, here, lfs.at[d - 1, h], lfr.at[d - 1, h], pdev).wait_recv()

            def middle():
                if h == 0 and d == 1:
                    pass_on(1)
                if h == 1:
                    settle(d, 0)
                    up_across(d)

            experts_on([(t, h * half, half), (q, h * half, half)], middle)
            pbuf[t, h * half : (h + 1) * half, :] = acc[0:half, :].astype(jnp.bfloat16)
            go(remote(half_of(pbuf, t, h), half_of(stage, d - 1, h), sts.at[d - 1, h],
                      str_.at[d - 1, h], pdev))
            far[h] = acc[half:, :]
        settle(d, 1)

    for d in range(columns):
        base = ex(back(d), c) * copies
        for y in range(1, teams):
            here = slab(ufull, base, lax.rem(g - y + teams, teams), copies)
            remote(here, here, uys.at[y - 1, d], uyr.at[y - 1, d], ydev(y)).wait_recv()
        go(remote(at(ufull, base, copies), at(ufull, base, copies), ucs.at[d], ucr.at[d], pdev))
    for d in range(columns):
        s = ex(back(d), 1 - c) * copies
        remote(at(ufull, s, copies), at(ufull, s, copies), ucs.at[d], ucr.at[d], pdev).wait_recv()
    remote(rbuf.at[0], rbuf.at[0], rs.at[0, 0], rr.at[0, 0], pdev).wait_recv()
    for h in range(2):
        span = slice(h * half, (h + 1) * half)
        total = own[span, :] + rbuf[0, span, :].astype(jnp.float32)
        for d in range(1, columns):
            here = half_of(rbuf, d, h)
            remote(here, here, rs.at[d, h], rr.at[d, h], xdev(d)).wait_recv()
            total = total + rbuf[d, span, :].astype(jnp.float32)
        out[span, :] = lax.dot_general(
            total.astype(jnp.bfloat16), ufull[...], (((1,), (1,)), ((), ())),
            preferred_element_type=jnp.float32,
        ).astype(jnp.bfloat16)
    for copy in sends:
        copy.wait_send()


def on_device(
    tokens, norm_gain, router, down_proj, up_proj, expert_gate, expert_up, expert_down,
    expert_ids, slot_pos, overflow_list,
):
    shards, copies = lax.axis_size("expert"), lax.axis_size("replica")
    teams = lax.axis_size("groups")
    columns = shards // CORES
    rows, width = tokens.shape
    latent = down_proj.shape[1]
    bf, f32 = jnp.bfloat16, jnp.float32
    dma = pltpu.SemaphoreType.DMA
    more = max(columns - 1, 1)
    extra = max(copies - 1, 1)
    anywhere, vmem = pl.BlockSpec(memory_space=pl.ANY), pl.BlockSpec(memory_space=pltpu.VMEM)
    return pl.pallas_call(
        functools.partial(layer, teams, shards, copies),
        out_shape=jax.ShapeDtypeStruct((rows, width), bf),
        in_specs=[anywhere, vmem, vmem] + [anywhere] * 5 + [vmem] * 3,
        out_specs=vmem,
        scratch_shapes=[
            pltpu.VMEM((rows, width), bf),
            pltpu.VMEM((rows, width), bf),
            pltpu.VMEM((width, latent), bf),
            pltpu.VMEM((width, latent), bf),
            pltpu.VMEM(expert_gate.shape, bf),
            pltpu.VMEM(expert_up.shape, bf),
            pltpu.VMEM(expert_down.shape, bf),
            pltpu.VMEM((shards, rows, latent), bf),
            pltpu.VMEM((shards, shards, pl.cdiv(expert_gate.shape[0], 8) * 8, rows), f32),
            pltpu.VMEM((rows, expert_gate.shape[2]), bf),
            pltpu.VMEM((rows, latent), f32),
            pltpu.VMEM((rows, latent), f32),
            pltpu.VMEM((shards, rows, latent), bf),
            pltpu.VMEM((columns, rows, latent), bf),
            pltpu.VMEM((rows, latent), bf),
            pltpu.VMEM((rows, pl.cdiv(expert_gate.shape[0], 8) * 8), f32),
            pltpu.VMEM((2, rows // 2, latent), f32),
            pltpu.VMEM((more, rows, latent), bf),
            dma((6,)),
            dma((extra,)), dma((extra,)),
            dma((more, copies)), dma((more, copies)),
            dma((columns, copies, 2)), dma((columns, copies, 2)),
            dma((columns, copies)), dma((columns, copies)),
            dma((extra, columns)), dma((extra, columns)),
            dma((more,)), dma((more,)),
            dma((columns,)), dma((columns,)),
            dma((max(teams - 1, 1), columns)), dma((max(teams - 1, 1), columns)),
            dma, dma, dma((more, 2)), dma((more, 2)), dma((more, 2)), dma((more, 2)),
            dma, dma, dma((more,)), dma((more,)), dma((more,)), dma((more,)),
            dma((columns, 2)), dma((columns, 2)), dma((more, 2)), dma((more, 2)),
        ],
        compiler_params=pltpu.CompilerParams(collective_id=0, has_side_effects=True,
                                             vmem_limit_bytes=60 * 1024 * 1024),
    )(
        tokens, norm_gain.reshape(1, -1), router.T, down_proj, up_proj, expert_gate, expert_up,
        expert_down, expert_ids.T, slot_pos.T, overflow_list,
    )


def solution(mesh):
    placed = (
        P(("groups", "expert", "replica"), None),
        P(),
        P(),
        P(("expert", "replica"), None),
        P(("expert", "replica"), None),
        P("expert", None, None),
        P("expert", None, None),
        P("expert", None, None),
        P(("groups", "expert", "replica"), None),
        P(("groups", "expert", "replica"), None),
        P(("groups", "expert", "replica"), None, None, None),
    )
    return jax.shard_map(
        on_device,
        mesh=mesh,
        in_specs=placed,
        out_specs=P(("groups", "expert", "replica"), None),
        check_vma=False,
    )
```

```python
import functools

import jax
import jax.numpy as jnp
from jax import lax
from jax.experimental import pallas as pl
from jax.experimental.pallas import tpu as pltpu
from jax.sharding import PartitionSpec as P

epsilon = 1e-06
CORES = 2
MESH = pl.DeviceIdType.MESH


def remote(src, dst, send, recv, where):
    return pltpu.make_async_remote_copy(
        src_ref=src, dst_ref=dst, send_sem=send, recv_sem=recv, device_id=where, device_id_type=MESH
    )


def layer(
    teams, shards, copies, tok, gain, router, down, up, wg, wu, wd, ids, slot, ov, out,
    tokv, normed, dfull, ufull, gv, uv, dv, lat, wts, hid, acc, own, pbuf, rbuf,
    rows_in, gate, far, stage,
    loc, dzs, dzr, dxs, dxr, dcs, dcr, dys, dyr, uzs, uzr, uxs, uxr, ucs, ucr, uys, uyr,
    lps, lpr, lxs, lxr, lfs, lfr, wps, wpr, wxs, wxr, wfs, wfr, rs, rr, sts, str_,
):
    columns = shards // CORES
    g, e, r = lax.axis_index("groups"), lax.axis_index("expert"), lax.axis_index("replica")
    x, c = e // CORES, e % CORES
    part = rows = down.shape[0]
    local = wg.shape[0]
    tokens = tok.shape[0]
    top = ids.shape[0]
    experts = router.shape[0]

    def ex(xx, cc):
        return xx * CORES + cc

    def back(d):
        return lax.rem(x - d + columns, columns)

    def fore(d):
        return lax.rem(x + d, columns)

    def zback(d):
        return lax.rem(r - d + copies, copies)

    def zdev(d):
        return {"replica": lax.rem(r + d, copies)}

    def xdev(d):
        return {"expert": ex(fore(d), c)}

    pdev = {"expert": ex(x, 1 - c)}

    def at(ref, index, n=1):
        return ref.at[pl.ds(pl.multiple_of(index * part, part), part * n), :]

    def ydev(d):
        return {"groups": lax.rem(g + d, teams)}

    share = up.shape[1] // teams

    lent = part // 2 // 16 * 16 if teams == 2 else 0
    kept = part - lent

    def fetched(ref, index):
        return ref.at[pl.ds(pl.multiple_of(index * part + g * lent, 16), kept), :]

    def swapped(index, team):
        return dfull.at[pl.ds(pl.multiple_of(index * part + team * kept, 16), lent), :]

    def slab(ref, index, team, n=1):
        return ref.at[
            pl.ds(pl.multiple_of(index * part, part), part * n),
            pl.ds(pl.multiple_of(team * share, share), share),
        ]

    barrier = pltpu.get_barrier_semaphore()
    count = 1
    pl.semaphore_signal(barrier, inc=1, device_id=pdev, device_id_type=MESH)
    for d in range(1, copies):
        pl.semaphore_signal(barrier, inc=1, device_id=zdev(d), device_id_type=MESH)
        count += 1
    for d in range(1, teams):
        pl.semaphore_signal(barrier, inc=1, device_id=ydev(d), device_id_type=MESH)
        count += 1
    for d in range(1, columns):
        for cc in (c, 1 - c):
            pl.semaphore_signal(
                barrier, inc=1, device_id={"expert": ex(fore(d), cc)}, device_id_type=MESH
            )
            count += 1
    tcopy = pltpu.make_async_copy(tok, tokv, loc.at[0])
    mine = e * copies + r
    dcopy = pltpu.make_async_copy(down, at(dfull, mine), loc.at[1])
    ucopy = pltpu.make_async_copy(slab(up, 0, g), slab(ufull, mine, g), loc.at[2])
    wcopies = [
        pltpu.make_async_copy(wg, gv, loc.at[3]),
        pltpu.make_async_copy(wu, uv, loc.at[4]),
        pltpu.make_async_copy(wd, dv, loc.at[5]),
    ]
    tcopy.start()
    dcopy.start()
    pl.semaphore_wait(barrier, count)

    sends = []

    def go(copy):
        copy.start()
        sends.append(copy)

    for d in range(1, columns):
        go(remote(fetched(down, 0), fetched(dfull, mine), dxs.at[d - 1, 0], dxr.at[d - 1, 0], xdev(d)))
    for d in range(1, copies):
        go(remote(fetched(down, 0), fetched(dfull, mine), dzs.at[d - 1], dzr.at[d - 1], zdev(d)))
    go(remote(down, at(dfull, mine), dcs.at[0, 0, 0], dcr.at[0, 0, 0], pdev))
    ucopy.start()
    for w in wcopies:
        w.start()

    tcopy.wait()
    step = 32

    @pl.loop(0, tokens // step)
    def _(i):
        at_rows = pl.ds(pl.multiple_of(i * step, step), step)
        v = tokv[at_rows, :].astype(jnp.float32)
        scaled = v * lax.rsqrt(jnp.mean(v * v, axis=-1, keepdims=True) + epsilon)
        normed[at_rows, :] = (scaled * gain[...]).astype(jnp.bfloat16)

    logits = lax.dot_general(
        router[...], normed[...], (((1,), (1,)), ((), ())), preferred_element_type=jnp.float32
    )
    sig = 1.0 / (1.0 + jnp.exp(-logits))
    expert = lax.broadcasted_iota(jnp.int32, (experts, tokens), 0)
    first = lax.broadcasted_iota(jnp.int32, (experts, tokens), 1) * top
    chosen = jnp.zeros((experts, tokens), jnp.float32)
    served = jnp.zeros((experts, tokens), jnp.float32)
    for k in range(top):
        hit = expert == ids[k : k + 1, :]
        chosen = jnp.where(hit, 1.0, chosen)
        served = jnp.where(hit & (slot[k : k + 1, :] >= 0), 1.0, served)
    listed = jnp.concatenate([ov[0, d] for d in range(shards)], axis=1).T
    for k in range(copies):
        entry = listed[:, k : k + 1]
        served = jnp.where((entry >= first) & (entry < first + top), 1.0, served)
    flipped = served * (sig / jnp.sum(chosen * sig, axis=0, keepdims=True))
    wts[e] = jnp.zeros(wts.shape[1:], jnp.float32)
    for d in range(shards):
        wts[e, d, 0:local, :] = flipped[d * local : (d + 1) * local, :]

    for d in range(1, columns):
        go(remote(wts.at[e], wts.at[e], wxs.at[d - 1], wxr.at[d - 1], xdev(d)))
    go(remote(wts.at[e], wts.at[e], wps, wpr, pdev))

    def down_on(d, j):
        s = ex(back(d), c) * copies + zback(j)
        here = fetched(dfull, s)
        go(remote(here, here, dcs.at[d, j, 0], dcr.at[d, j, 0], pdev))
        if lent:
            here = swapped(s, g)
            go(remote(here, here, dys.at[d, j], dyr.at[d, j], ydev(1)))

    def down_z(j):
        here = fetched(dfull, e * copies + zback(j))
        remote(here, here, dzs.at[j - 1], dzr.at[j - 1], zdev(j)).wait_recv()
        for d in range(1, columns):
            go(remote(here, here, dxs.at[d - 1, j], dxr.at[d - 1, j], xdev(d)))
        down_on(0, j)

    def down_x(j):
        for d in range(1, columns):
            here = fetched(dfull, ex(back(d), c) * copies + zback(j))
            remote(here, here, dxs.at[d - 1, j], dxr.at[d - 1, j], xdev(d)).wait_recv()
            down_on(d, j)

    for j in range(1, copies):
        down_z(j)
        down_x(j - 1)
    for d in range(1, columns):
        go(remote(slab(up, 0, g), slab(ufull, mine, g), uxs.at[d - 1], uxr.at[d - 1], xdev(d)))
    ucopy.wait()
    for z in range(1, copies):
        here = slab(ufull, mine, g)
        go(remote(here, here, uzs.at[z - 1, 0], uzr.at[z - 1, 0], zdev(z)))
    down_x(copies - 1)
    others = [(d, j) for d in range(columns) for j in range(copies) if d + j]
    if lent:
        for d, j in others:
            here = swapped(ex(back(d), c) * copies + zback(j), 1 - g)
            remote(here, here, dys.at[d, j], dyr.at[d, j], ydev(1)).wait_recv()
            go(remote(here, here, dcs.at[d, j, 1], dcr.at[d, j, 1], pdev))
    dcopy.wait()
    here = at(dfull, ex(x, 1 - c) * copies + r)
    remote(here, here, dcs.at[0, 0, 0], dcr.at[0, 0, 0], pdev).wait_recv()
    for d, j in others:
        s = ex(back(d), 1 - c) * copies + zback(j)
        here = fetched(dfull, s)
        remote(here, here, dcs.at[d, j, 0], dcr.at[d, j, 0], pdev).wait_recv()
        if lent:
            here = swapped(s, 1 - g)
            remote(here, here, dcs.at[d, j, 1], dcr.at[d, j, 1], pdev).wait_recv()

    half = tokens // 2

    def half_of(ref, index, h):
        return ref.at[index, pl.ds(h * half, half), :]

    for h in range(2):
        span = slice(h * half, (h + 1) * half)
        lat[e, span, :] = jnp.dot(
            normed[span, :], dfull[...], preferred_element_type=jnp.float32
        ).astype(jnp.bfloat16)
        for d in range(1, columns):
            here = half_of(lat, e, h)
            go(remote(here, here, lxs.at[d - 1, h], lxr.at[d - 1, h], xdev(d)))
    go(remote(lat.at[e], lat.at[e], lps, lpr, pdev))

    for d in range(1, columns):
        here = slab(ufull, ex(back(d), c) * copies + r, g)
        remote(here, here, uxs.at[d - 1], uxr.at[d - 1], xdev(d)).wait_recv()
        for z in range(1, copies):
            go(remote(here, here, uzs.at[z - 1, d], uzr.at[z - 1, d], zdev(z)))

    def up_across(d):
        base = ex(back(d), c) * copies
        for z in range(1, copies):
            here = slab(ufull, base + zback(z), g)
            remote(here, here, uzs.at[z - 1, d], uzr.at[z - 1, d], zdev(z)).wait_recv()
        here = slab(ufull, base, g, copies)
        for y in range(1, teams):
            go(remote(here, here, uys.at[y - 1, d], uyr.at[y - 1, d], ydev(y)))

    width = wg.shape[2]
    piece = 256

    def experts_on(pieces, middle):
        block = [lat[which, lo : lo + n, :] for which, lo, n in pieces]
        rows_in[...] = block[0] if len(block) == 1 else jnp.concatenate(block, axis=0)
        scale = [wts[which, e].T[lo : lo + n] for which, lo, n in pieces]
        gate[...] = scale[0] if len(scale) == 1 else jnp.concatenate(scale, axis=0)
        acc[...] = jnp.zeros_like(acc)

        def one(n):
            inner = rows_in[...]
            spot = lax.broadcasted_iota(jnp.int32, gate.shape, 1)
            weights = jnp.sum(jnp.where(spot == n, gate[...], 0.0), axis=1, keepdims=True)
            for f in range(0, width, piece):
                a = jnp.dot(inner, gv[n, :, f : f + piece], preferred_element_type=jnp.float32)
                b = jnp.dot(inner, uv[n, :, f : f + piece], preferred_element_type=jnp.float32)
                h = a / (1.0 + jnp.exp(-a)) * b * weights
                hid[:, f : f + piece] = h.astype(jnp.bfloat16)
            acc[...] += jnp.dot(hid[...], dv[n], preferred_element_type=jnp.float32)

        pl.loop(0, local // 2)(one)
        middle()
        pl.loop(local // 2, local)(one)

    def pass_on(h):
        for d in range(1, columns):
            q = ex(back(d), c)
            if h == 0:
                remote(wts.at[q], wts.at[q], wxs.at[d - 1], wxr.at[d - 1], xdev(d)).wait_recv()
                go(remote(wts.at[q], wts.at[q], wfs.at[d - 1], wfr.at[d - 1], pdev))
            here = half_of(lat, q, h)
            remote(here, here, lxs.at[d - 1, h], lxr.at[d - 1, h], xdev(d)).wait_recv()
            go(remote(here, here, lfs.at[d - 1, h], lfr.at[d - 1, h], pdev))

    for w in wcopies:
        w.wait()
    experts_on([(e, 0, tokens)], lambda: None)
    own[...] = acc[...]
    p = ex(x, 1 - c)
    remote(wts.at[p], wts.at[p], wps, wpr, pdev).wait_recv()
    remote(lat.at[p], lat.at[p], lps, lpr, pdev).wait_recv()
    experts_on([(p, 0, tokens)], lambda: pass_on(0))
    pbuf[p] = acc[...].astype(jnp.bfloat16)
    go(remote(pbuf.at[p], rbuf.at[0], rs.at[0, 0], rr.at[0, 0], pdev))
    up_across(0)

    def settle(d, h):
        span = slice(h * half, (h + 1) * half)
        q = ex(back(d), c)
        here = half_of(stage, d - 1, h)
        remote(here, here, sts.at[d - 1, h], str_.at[d - 1, h], pdev).wait_recv()
        total = far[h] + stage[d - 1, span, :].astype(jnp.float32)
        pbuf[q, span, :] = total.astype(jnp.bfloat16)
        go(remote(half_of(pbuf, q, h), half_of(rbuf, d, h), rs.at[d, h], rr.at[d, h], {"expert": q}))

    for d in range(1, columns):
        q, t = ex(back(d), c), ex(back(d), 1 - c)
        for h in range(2):
            if h == 0:
                remote(wts.at[t], wts.at[t], wfs.at[d - 1], wfr.at[d - 1], pdev).wait_recv()
            here = half_of(lat, t, h)
            remote(here, here, lfs.at[d - 1, h], lfr.at[d - 1, h], pdev).wait_recv()

            def middle():
                if h == 0 and d == 1:
                    pass_on(1)
                if h == 1:
                    settle(d, 0)
                    up_across(d)

            experts_on([(t, h * half, half), (q, h * half, half)], middle)
            pbuf[t, h * half : (h + 1) * half, :] = acc[0:half, :].astype(jnp.bfloat16)
            go(remote(half_of(pbuf, t, h), half_of(stage, d - 1, h), sts.at[d - 1, h],
                      str_.at[d - 1, h], pdev))
            far[h] = acc[half:, :]
        settle(d, 1)

    for d in range(columns):
        base = ex(back(d), c) * copies
        for y in range(1, teams):
            here = slab(ufull, base, lax.rem(g - y + teams, teams), copies)
            remote(here, here, uys.at[y - 1, d], uyr.at[y - 1, d], ydev(y)).wait_recv()
        go(remote(at(ufull, base, copies), at(ufull, base, copies), ucs.at[d], ucr.at[d], pdev))
    for d in range(columns):
        s = ex(back(d), 1 - c) * copies
        remote(at(ufull, s, copies), at(ufull, s, copies), ucs.at[d], ucr.at[d], pdev).wait_recv()
    remote(rbuf.at[0], rbuf.at[0], rs.at[0, 0], rr.at[0, 0], pdev).wait_recv()
    for h in range(2):
        span = slice(h * half, (h + 1) * half)
        total = own[span, :] + rbuf[0, span, :].astype(jnp.float32)
        for d in range(1, columns):
            here = half_of(rbuf, d, h)
            remote(here, here, rs.at[d, h], rr.at[d, h], xdev(d)).wait_recv()
            total = total + rbuf[d, span, :].astype(jnp.float32)
        out[span, :] = lax.dot_general(
            total.astype(jnp.bfloat16), ufull[...], (((1,), (1,)), ((), ())),
            preferred_element_type=jnp.float32,
        ).astype(jnp.bfloat16)
    for copy in sends:
        copy.wait_send()


def on_device(
    tokens, norm_gain, router, down_proj, up_proj, expert_gate, expert_up, expert_down,
    expert_ids, slot_pos, overflow_list,
):
    shards, copies = lax.axis_size("expert"), lax.axis_size("replica")
    teams = lax.axis_size("groups")
    columns = shards // CORES
    rows, width = tokens.shape
    latent = down_proj.shape[1]
    bf, f32 = jnp.bfloat16, jnp.float32
    dma = pltpu.SemaphoreType.DMA
    more = max(columns - 1, 1)
    extra = max(copies - 1, 1)
    anywhere, vmem = pl.BlockSpec(memory_space=pl.ANY), pl.BlockSpec(memory_space=pltpu.VMEM)
    return pl.pallas_call(
        functools.partial(layer, teams, shards, copies),
        out_shape=jax.ShapeDtypeStruct((rows, width), bf),
        in_specs=[anywhere, vmem, vmem] + [anywhere] * 5 + [vmem] * 3,
        out_specs=vmem,
        scratch_shapes=[
            pltpu.VMEM((rows, width), bf),
            pltpu.VMEM((rows, width), bf),
            pltpu.VMEM((width, latent), bf),
            pltpu.VMEM((width, latent), bf),
            pltpu.VMEM(expert_gate.shape, bf),
            pltpu.VMEM(expert_up.shape, bf),
            pltpu.VMEM(expert_down.shape, bf),
            pltpu.VMEM((shards, rows, latent), bf),
            pltpu.VMEM((shards, shards, pl.cdiv(expert_gate.shape[0], 8) * 8, rows), f32),
            pltpu.VMEM((rows, expert_gate.shape[2]), bf),
            pltpu.VMEM((rows, latent), f32),
            pltpu.VMEM((rows, latent), f32),
            pltpu.VMEM((shards, rows, latent), bf),
            pltpu.VMEM((columns, rows, latent), bf),
            pltpu.VMEM((rows, latent), bf),
            pltpu.VMEM((rows, pl.cdiv(expert_gate.shape[0], 8) * 8), f32),
            pltpu.VMEM((2, rows // 2, latent), f32),
            pltpu.VMEM((more, rows, latent), bf),
            dma((6,)),
            dma((extra,)), dma((extra,)),
            dma((more, copies)), dma((more, copies)),
            dma((columns, copies, 2)), dma((columns, copies, 2)),
            dma((columns, copies)), dma((columns, copies)),
            dma((extra, columns)), dma((extra, columns)),
            dma((more,)), dma((more,)),
            dma((columns,)), dma((columns,)),
            dma((max(teams - 1, 1), columns)), dma((max(teams - 1, 1), columns)),
            dma, dma, dma((more, 2)), dma((more, 2)), dma((more, 2)), dma((more, 2)),
            dma, dma, dma((more,)), dma((more,)), dma((more,)), dma((more,)),
            dma((columns, 2)), dma((columns, 2)), dma((more, 2)), dma((more, 2)),
        ],
        compiler_params=pltpu.CompilerParams(collective_id=0, has_side_effects=True,
                                             vmem_limit_bytes=60 * 1024 * 1024),
    )(
        tokens, norm_gain.reshape(1, -1), router.T, down_proj, up_proj, expert_gate, expert_up,
        expert_down, expert_ids.T, slot_pos.T, overflow_list,
    )


def solution(mesh):
    placed = (
        P(("groups", "expert", "replica"), None),
        P(),
        P(),
        P(("expert", "replica"), None),
        P(("expert", "replica"), None),
        P("expert", None, None),
        P("expert", None, None),
        P("expert", None, None),
        P(("groups", "expert", "replica"), None),
        P(("groups", "expert", "replica"), None),
        P(("groups", "expert", "replica"), None, None, None),
    )
    return jax.shard_map(
        on_device,
        mesh=mesh,
        in_specs=placed,
        out_specs=P(("groups", "expert", "replica"), None),
        check_vma=False,
    )
```
